256 devices in a mesh: dp: 4 (over y), mp: 64 (over x, z, core).
Axes of the slice: x: 4, y: 4, z: 8, core: 2. Of those that a mesh axis runs over, the one named last changes fastest.
Arguments:
- inputs: bfloat16 [8, 256, 6144], P('dp', None, 'mp'), may hold values from -6 to 6
- cotangent: bfloat16 [8, 256, 6144], P('dp', None, 'mp'), may hold values from -6 to 6
- w_up: bfloat16 [6144, 24576], P('dp', 'mp'), may hold values from -0.078125 to 0.078125
- w_down: bfloat16 [24576, 6144], P('mp', 'dp'), may hold values from -0.0390625 to 0.0390625
- thresholds: float32 [2], replicated, may hold values from 23592.96 to 58982.4
Outputs:
- grad_up: float32 [6144, 24576], P('dp', 'mp')
- grad_down: float32 [24576, 6144], P('mp', 'dp')
- norms: float32 [8, 2], P('dp')
The draws below stay inside these ranges and needn't reach their ends.
All inputs are finite; a program needn't handle non-finite values.
Results may differ from the reference program's by a relative error of at most 0.0085.
Values may be sent and summed in bfloat16 or wider, within the bound.
A program may use at most 128 MiB of HBM per device.

```python
import math
import jax
import jax.numpy as jnp
from jax import lax

D = 6144
FF = 24576
P_SIZE = 256
IMG_DEV = 2
IMAGES = 8
N_DP = 4


def patch_field(key, window):
    random_part = jax.random.normal(key, (IMAGES, P_SIZE, D), jnp.float32)
    summed = jnp.zeros((IMAGES, P_SIZE, D), jnp.float32)
    for offset in range(window):
        summed = summed + jnp.roll(random_part, offset, axis=1)
    return summed / math.sqrt(window)


def drawn_field(key):
    key_base, key_smooth = jax.random.split(key)
    rough_part = jax.random.normal(key_base, (IMAGES, P_SIZE, D), jnp.float32)
    smooth = patch_field(key_smooth, max(2, P_SIZE // 16))
    return jnp.clip(0.7071 * rough_part + 0.7071 * smooth, -6.0, 6.0)


def draw_inputs(key, part):
    field_key = jax.random.fold_in(key, 29)
    blended = drawn_field(field_key)
    return blended.astype(jnp.bfloat16)


def draw_cotangent(key, part):
    key_field, key_order, key_jitter = jax.random.split(jax.random.fold_in(key, 17), 3)
    ranking = jax.random.permutation(key_order, IMAGES).astype(jnp.float32)
    jitter = jax.random.uniform(key_jitter, (IMAGES,), jnp.float32, 0.0, 1.0)
    scales = jnp.exp(math.log(0.05) + (ranking + jitter) / IMAGES * math.log(20.0)).reshape(IMAGES, 1, 1)
    blended = drawn_field(key_field)
    return (blended * scales).astype(jnp.bfloat16)


def steps_of(key, dims, cuts, smallest, high):
    factor_of, own = 1.0, jax.random.fold_in(key, 6)
    for axis_at, shards_of in cuts:
        steps = jnp.exp(jax.random.uniform(jax.random.fold_in(own, axis_at), (shards_of,), jnp.float32, smallest / len(cuts), high / len(cuts)))
        factor_of = factor_of * jnp.repeat(steps, dims[axis_at] // shards_of).reshape([-1 if axis == axis_at else 1 for axis in range(len(dims))])
    return factor_of


def gaussian(key, shape, scale, bound, cuts=(), dtype=jnp.bfloat16):
    values = jax.random.normal(key, shape, jnp.float32) * scale
    if len(cuts) > 0:
        values = steps_of(key, shape, cuts, -0.22, 0.18) * values
    return jnp.clip(values, min=-bound, max=bound).astype(dtype)


def setup_inputs(seed: int = 0) -> dict:
    streams_of = jax.random.split(jax.random.key(seed), 6)
    inputs = draw_inputs(jax.random.fold_in(streams_of[5], 71), 0)
    cotangent = draw_cotangent(jax.random.fold_in(streams_of[5], 71), 0)
    w_up = gaussian(streams_of[2], (D, FF), D ** -0.5, 0.078125, ((0, 4), (1, 64)))
    w_down = gaussian(streams_of[3], (FF, D), FF ** -0.5, 0.0390625, ((0, 64), (1, 4)))
    thresholds = jnp.clip(jnp.exp(jax.random.uniform(streams_of[4], (2,), jnp.float32, math.log(23592.96), math.log(58982.4))), 23592.96, 58982.4)
    return {"inputs": inputs, "cotangent": cotangent, "w_up": w_up, "w_down": w_down, "thresholds": thresholds}


inv_root_two = 0.7071067811865476
inv_root_two_pi = 0.3989422804014327

def normal_cdf(value):
    return 0.5 * (1.0 + lax.erf(value * inv_root_two))

def gram_of(array):
    cube = array.reshape(IMAGES, P_SIZE, -1).astype(jnp.float32)
    return jnp.einsum('btd,bsd->bts', cube, cube, precision=lax.Precision.HIGHEST)

def group_sum(left, right):
    left_groups = left.reshape(N_DP, IMG_DEV * P_SIZE, left.shape[1])
    right_groups = right.reshape(N_DP, IMG_DEV * P_SIZE, right.shape[1])

    def add_group(total, pair):
        term = lax.dot_general(pair[0], pair[1], (((0,), (0,)), ((), ())), preferred_element_type=jnp.float32)
        rounded = lax.optimization_barrier(term.astype(jnp.bfloat16))
        return (total + rounded.astype(jnp.float32), None)
    start = jnp.zeros((left.shape[1], right.shape[1]), jnp.float32)
    total, _ = lax.scan(add_group, start, (left_groups, right_groups))
    return total

def reference(inputs, cotangent, w_up, w_down, thresholds):
    rows = inputs.reshape(IMAGES * P_SIZE, D)
    dy_rows = cotangent.reshape(IMAGES * P_SIZE, D)
    pre = jnp.dot(rows, w_up, preferred_element_type=jnp.float32)
    act = (pre * normal_cdf(pre)).astype(jnp.bfloat16)
    dact = jnp.dot(dy_rows, w_down.T, preferred_element_type=jnp.float32)
    slope = normal_cdf(pre) + pre * jnp.exp(-0.5 * pre * pre) * inv_root_two_pi
    dpre = (dact * slope).astype(jnp.bfloat16)
    sq_up = lax.optimization_barrier(jnp.sum(gram_of(rows) * gram_of(dpre), axis=(1, 2)))
    sq_down = lax.optimization_barrier(jnp.sum(gram_of(act) * gram_of(dy_rows), axis=(1, 2)))
    norms = jnp.stack([jnp.sqrt(sq_up), jnp.sqrt(sq_down)], axis=1)
    factor = jnp.minimum(1.0, thresholds[None, :] / (norms + 1e-06))
    dpre_clip = (factor[:, 0][:, None, None] * dpre.reshape(IMAGES, P_SIZE, FF).astype(jnp.float32)).astype(jnp.bfloat16).reshape(IMAGES * P_SIZE, FF)
    cot_clip = (factor[:, 1][:, None, None] * cotangent.astype(jnp.float32)).astype(jnp.bfloat16).reshape(IMAGES * P_SIZE, D)
    grad_up = group_sum(rows, dpre_clip)
    grad_down = group_sum(act, cot_clip)
    return (grad_up, grad_down, norms)
```

```python
import jax
import jax.numpy as jnp
from jax import lax
from jax.experimental import pallas as pl
from jax.experimental.pallas import tpu as pltpu
from jax.sharding import PartitionSpec as P

inv_root_two = 0.7071067811865476
inv_root_two_pi = 0.3989422804014327

F32, BF16 = jnp.float32, jnp.bfloat16
NX, NY, NZ, NC = 4, 4, 8, 2
IMGS, PATCHES, FEATS = 2, 256, 96
DEPTH, HIDDEN = 1536, 384
HALF = HIDDEN // 2
WIDE = NY * PATCHES
COUNT = NY * IMGS
PEERS = 15
NT = (((1,), (1,)), ((), ()))


def normal_cdf(value):
    return 0.5 * (1.0 + lax.erf(value * inv_root_two))


def mod(value, size):
    return lax.rem(value + size, size)


def kernel(
    x_in, dy_in, w_up, w_down, thresholds,
    grad_up, grad_down, norms_out,
    w_raw, w_rows, full, part, own, relay, got, slope, spread, image_up, image_down,
    sum_up, sum_down, squares, middle, heard, factors, lengths,
    local_sem, first_send, first_self, first_recv, ring_send, ring_recv, twin_send, twin_recv,
    rs_send, rs_recv, ag_send, ag_recv, norm_send, norm_recv, out_sem,
):
    y, m = lax.axis_index("dp"), lax.axis_index("mp")
    c, z, x = lax.rem(m, NC), lax.rem(lax.div(m, NC), NZ), lax.div(m, NC * NZ)

    def device(yy, xx, zz, cc):
        return (yy, (xx * NZ + zz) * NC + cc)

    def plane_peer(k):
        return device(mod(y + k // NX, NY), mod(x + k % NX, NX), z, c)

    def line_peer(k):
        return device(y, x, mod(z + k // NC, NZ), mod(c + k % NC, NC))

    right, left = device(y, x, mod(z + 1, NZ), c), device(y, x, mod(z - 1, NZ), c)
    twin = device(y, x, z, 1 - c)
    above, below = mod(y + 1, NY), mod(y - 1, NY)
    up, down = device(above, x, z, c), device(below, x, z, c)

    def send(src, dst, send_sem, recv_sem, target):
        pltpu.make_async_remote_copy(
            src_ref=src, dst_ref=dst, send_sem=send_sem, recv_sem=recv_sem,
            device_id=target, device_id_type=pl.DeviceIdType.MESH,
        ).start()

    def wait(ref, sem):
        pltpu.make_async_copy(ref, ref, sem).wait()

    up_copy = pltpu.make_async_copy(w_up, w_raw, local_sem.at[0])
    down_copy = pltpu.make_async_copy(w_down, w_rows.at[1], local_sem.at[1])
    up_copy.start()
    down_copy.start()

    barrier = pltpu.get_barrier_semaphore()
    for k in range(1, PEERS + 1):
        for target in (plane_peer(k), line_peer(k)):
            pl.semaphore_signal(
                barrier, inc=1, device_id=target, device_id_type=pl.DeviceIdType.MESH
            )
    pl.semaphore_wait(barrier, 2 * PEERS)

    own_rows = pl.ds(pl.multiple_of((z * NC + c) * FEATS, FEATS), FEATS)
    own_cols = pl.ds(pl.multiple_of(y * PATCHES, PATCHES), PATCHES)
    for t, src in enumerate((x_in, dy_in)):
        for h in range(IMGS):
            dst = full.at[t, h, own_rows, own_cols]
            for k in range(1, NX):
                send(
                    src.at[h], dst, first_send.at[t, h], first_recv.at[t, h],
                    device(x, mod(x + k, NX), z, c),
                )

            @pl.when(x != y)
            def _():
                send(
                    src.at[h], dst, first_self.at[t, h], first_recv.at[t, h], device(x, x, z, c)
                )

            @pl.when(x == y)
            def _():
                pltpu.make_async_copy(src.at[h], dst, first_recv.at[t, h]).start()

    up_copy.wait()
    for k in range(DEPTH // PATCHES):
        span = slice(k * PATCHES, (k + 1) * PATCHES)
        w_rows[0, :, span] = w_raw[span, :].T
    down_copy.wait()

    def chunk(t, h, zz, cols=slice(None)):
        return full.at[t, h, pl.ds(pl.multiple_of((zz * NC + c) * FEATS, FEATS), FEATS), cols]

    def to_twin(t, h, ref):
        send(ref, ref, twin_send.at[t, h], twin_recv.at[t, h], twin)

    def halves(s):
        last = s == NZ // 2 - 1
        return (slice(0, WIDE // 2), slice(WIDE // 2, WIDE)) if last else (slice(None),) * 2

    def ring_step(t, h, s):
        first, second = halves(s)
        ref = chunk(t, h, mod(z - s, NZ), first)
        send(ref, ref, ring_send.at[t, h, 0], ring_recv.at[t, h, 0, s], right)
        ref = chunk(t, h, mod(z + s, NZ), second)
        send(ref, ref, ring_send.at[t, h, 1], ring_recv.at[t, h, 1, s], left)

    def ring_open(t, h):
        mine = full.at[t, h, own_rows, :]
        wait(mine, first_recv.at[t, h])
        ring_step(t, h, 0)
        to_twin(t, h, mine)

    def ring_take(t, h, s):
        first, second = halves(s)
        from_left = chunk(t, h, mod(z - 1 - s, NZ), first)
        from_right = chunk(t, h, mod(z + 1 + s, NZ), second)
        wait(from_left, ring_recv.at[t, h, 0, s])
        wait(from_right, ring_recv.at[t, h, 1, s])
        if s < NZ // 2 - 1:
            ring_step(t, h, s + 1)
        to_twin(t, h, from_left)
        to_twin(t, h, from_right)

    def gathered(t, h):
        wait(full.at[t, h, pl.ds(0, DEPTH // 2), :], twin_recv.at[t, h])

    low, high = slice(0, HALF), slice(HALF, HIDDEN)

    def partials(t, h):
        def body(i, carry):
            shift = jnp.where(i == 0, 2, jnp.where(i == 1, 1, jnp.where(i == 2, 3, 0)))
            owner = lax.rem(y + shift, NY)
            cols = pl.ds(pl.multiple_of(owner * PATCHES, PATCHES), PATCHES)
            value = jnp.dot(w_rows[t], full[t, h, :, cols], preferred_element_type=F32)
            part[t, h, i] = value.astype(BF16)
            own[t, h] = value

            @pl.when(i == 0)
            def _():
                send(
                    part.at[t, h, 0, low, :], relay.at[t, h, 0],
                    rs_send.at[t, h, 0], rs_recv.at[t, h, 0, 0], up,
                )
                send(
                    part.at[t, h, 0, high, :], relay.at[t, h, 1],
                    rs_send.at[t, h, 1], rs_recv.at[t, h, 1, 0], down,
                )

            @pl.when(i == 1)
            def _():
                send(
                    part.at[t, h, 1, high, :], got.at[t, h, 0, high, :],
                    rs_send.at[t, h, 0], rs_recv.at[t, h, 0, 1], up,
                )

            @pl.when(i == 2)
            def _():
                send(
                    part.at[t, h, 2, low, :], got.at[t, h, 1, low, :],
                    rs_send.at[t, h, 1], rs_recv.at[t, h, 1, 1], down,
                )

            return carry

        lax.fori_loop(0, NY, body, 0)

    def relay_partials(t, h):
        for d, (i, rows, target) in enumerate(((1, low, up), (2, high, down))):
            wait(relay.at[t, h, d], rs_recv.at[t, h, d, 0])
            both = part[t, h, i, rows, :].astype(F32) + relay[t, h, d].astype(F32)
            part[t, h, i, rows, :] = both.astype(BF16)
            send(
                part.at[t, h, i, rows, :], got.at[t, h, d, rows, :],
                rs_send.at[t, h, d], rs_recv.at[t, h, d, 2], target,
            )

    def received(t, h):
        wait(got.at[t, h, 0, high, :], rs_recv.at[t, h, 0, 1])
        wait(got.at[t, h, 1, low, :], rs_recv.at[t, h, 1, 1])
        wait(got.at[t, h, 0, low, :], rs_recv.at[t, h, 0, 2])
        wait(got.at[t, h, 1, high, :], rs_recv.at[t, h, 1, 2])

    BAND = 48

    def banded(fn):
        def body(b, carry):
            fn(pl.ds(pl.multiple_of(b * BAND, BAND), BAND))
            return carry

        lax.fori_loop(0, HIDDEN // BAND, body, 0)

    def total(t, h, rows):
        return (
            own[t, h, rows, :]
            + got[t, h, 0, rows, :].astype(F32)
            + got[t, h, 1, rows, :].astype(F32)
        )

    def activate(h):
        def body(rows):
            pre = total(0, h, rows)
            cdf = normal_cdf(pre)
            spread[0, h, y, rows, :] = (pre * cdf).astype(BF16)
            slope[h, rows, :] = cdf + pre * jnp.exp(-0.5 * pre * pre) * inv_root_two_pi

        banded(body)

    def descend(h):
        def body(rows):
            spread[1, h, y, rows, :] = (total(1, h, rows) * slope[h, rows, :]).astype(BF16)

        banded(body)

    def spread_step(t, h, d, j, owner, rows):
        ref = spread.at[t, h, owner, rows, :]
        send(ref, ref, ag_send.at[t, h, d], ag_recv.at[t, h, d, j], (up, down)[d])

    def spread_open(t, h):
        spread_step(t, h, 0, 0, y, low)
        spread_step(t, h, 1, 0, y, high)
        spread_step(t, h, 0, 1, y, high)
        spread_step(t, h, 1, 1, y, low)

    def spread_relay(t, h):
        wait(spread.at[t, h, below, low, :], ag_recv.at[t, h, 0, 0])
        spread_step(t, h, 0, 2, below, low)
        wait(spread.at[t, h, above, high, :], ag_recv.at[t, h, 1, 0])
        spread_step(t, h, 1, 2, above, high)

    def spread_near(t, h):
        wait(spread.at[t, h, below, high, :], ag_recv.at[t, h, 0, 1])
        wait(spread.at[t, h, above, low, :], ag_recv.at[t, h, 1, 1])

    def spread_far(t, h):
        far = mod(y + 2, NY)
        wait(spread.at[t, h, far, low, :], ag_recv.at[t, h, 0, 2])
        wait(spread.at[t, h, far, high, :], ag_recv.at[t, h, 1, 2])

    BLOCK = 512

    def fold(value):
        parts = [value[:, k : k + 128] for k in range(0, value.shape[1], 128)]
        return sum(parts[1:], parts[0])

    def image_of(t, h, owner):
        cols = pl.ds(pl.multiple_of(owner * PATCHES, PATCHES), PATCHES)
        index = owner * IMGS + h

        def body(b, carry):
            span = pl.ds(pl.multiple_of(b * BLOCK, BLOCK), BLOCK)
            if t == 0:
                value = lax.dot_general(
                    full[0, h, span, cols], spread[1, h, owner], NT, preferred_element_type=F32
                )
                image_up[index, span, :] = value.astype(BF16)
            else:
                value = lax.dot_general(
                    spread[0, h, owner], full[1, h, span, cols], NT, preferred_element_type=F32
                )
                image_down[index, :, span] = value.astype(BF16)
            return carry + fold(jnp.sum(value * value, axis=0, keepdims=True))

        start = jnp.zeros((1, 128), F32)
        squares[t, pl.ds(index, 1), :] = lax.fori_loop(0, DEPTH // BLOCK, body, start)

    def all_images(t, h):
        def body(i, carry):
            image_of(t, h, lax.rem(y + i, NY))
            return carry

        lax.fori_loop(0, NY, body, 0)

    def images_as_they_come(h):
        def body(i, carry):
            @pl.when(i == 1)
            def _():
                spread_relay(1, h)
                spread_near(1, h)

            @pl.when(i == 3)
            def _():
                spread_far(1, h)

            shift = jnp.where(i == 0, 0, jnp.where(i == 1, 1, jnp.where(i == 2, 3, 2)))
            image_of(0, h, lax.rem(y + shift, NY))
            return carry

        lax.fori_loop(0, NY, body, 0)

    def norm_open(t):
        for k in range(1, PEERS + 1):
            send(
                squares.at[t], heard.at[t, 0, k - 1],
                norm_send.at[t, 0], norm_recv.at[t, 0], plane_peer(k),
            )

    def norm_middle(t):
        wait(heard.at[t, 0], norm_recv.at[t, 0])
        middle[t] = squares[t] + jnp.sum(heard[t, 0], axis=0)
        for k in range(1, PEERS + 1):
            send(
                middle.at[t], heard.at[t, 1, k - 1],
                norm_send.at[t, 1], norm_recv.at[t, 1], line_peer(k),
            )

    def norm_close(t):
        wait(heard.at[t, 1], norm_recv.at[t, 1])
        lanes = middle[t] + jnp.sum(heard[t, 1], axis=0)
        length = jnp.sqrt(jnp.sum(lanes, axis=1, keepdims=True))
        factor = jnp.minimum(1.0, thresholds[t] / (length + 1e-06))
        lengths[t] = jnp.broadcast_to(length, (COUNT, 128))
        factors[t] = jnp.broadcast_to(factor, (COUNT, 128))

    def combine(t, images, sums, out, rows_each, pieces):
        size = sums.shape[0] // pieces
        for p in range(pieces):

            def body(b, carry):
                start = p * size + b * rows_each
                rows = pl.ds(pl.multiple_of(start, rows_each), rows_each)
                for k in range(0, sums.shape[1], 384):
                    cols = slice(k, k + 384)
                    acc = None
                    for i in range(COUNT):
                        factor = jnp.tile(factors[t, i : i + 1, :], (1, 3))
                        term = images[i, rows, cols].astype(F32) * factor
                        acc = term if acc is None else acc + term
                    sums[rows, cols] = acc
                return carry

            lax.fori_loop(0, size // rows_each, body, 0)
            rows = slice(p * size, (p + 1) * size)
            pltpu.make_async_copy(sums.at[rows, :], out.at[rows, :], out_sem.at[t, p]).start()

    def combine_wait(t, sums, out, pieces):
        size = sums.shape[0] // pieces
        for p in range(pieces):
            rows = slice(p * size, (p + 1) * size)
            pltpu.make_async_copy(sums.at[rows, :], out.at[rows, :], out_sem.at[t, p]).wait()

    steps = NZ // 2
    for h in range(IMGS):
        ring_open(0, h)
    for s in range(steps - 1):
        for h in range(IMGS):
            ring_take(0, h, s)
    for h in range(IMGS):
        ring_open(1, h)
    for h in range(IMGS):
        ring_take(0, h, steps - 1)
    for h in range(IMGS):
        gathered(0, h)
        partials(0, h)
    relay_partials(0, 0)
    relay_partials(0, 1)
    for h in range(IMGS):
        ring_take(1, h, 0)
    for h in range(IMGS):
        received(0, h)
        activate(h)
        spread_open(0, h)
    for h in range(IMGS):
        ring_take(1, h, 1)
    for h in range(IMGS):
        spread_relay(0, h)
    for h in range(IMGS):
        ring_take(1, h, 2)
    for h in range(IMGS):
        ring_take(1, h, 3)
    for h in range(IMGS):
        spread_near(0, h)
        spread_far(0, h)
    for h in range(IMGS):
        gathered(1, h)
        partials(1, h)
    relay_partials(1, 0)
    all_images(1, 0)
    relay_partials(1, 1)
    received(1, 0)
    descend(0)
    spread_open(1, 0)
    all_images(1, 1)
    received(1, 1)
    descend(1)
    spread_open(1, 1)
    norm_open(1)
    images_as_they_come(0)
    norm_middle(1)
    images_as_they_come(1)
    norm_open(0)
    norm_close(1)
    combine(1, image_down, sum_down, grad_down, 16, 2)
    norm_middle(0)
    norm_close(0)
    combine(0, image_up, sum_up, grad_up, 16, 4)

    mine = pl.ds(y * IMGS, IMGS)
    lane = lax.broadcasted_iota(jnp.int32, (IMGS, 128), 1)
    both = jnp.where(lane == 0, lengths[0, mine, :], lengths[1, mine, :])
    norms_out[...] = both[:, :2]

    for t in range(2):
        for h in range(IMGS):
            wait(full.at[t, h, pl.ds(0, FEATS), pl.ds(0, 3 * PATCHES)], first_send.at[t, h])

            @pl.when(x != y)
            def _():
                wait(full.at[t, h, pl.ds(0, FEATS), pl.ds(0, PATCHES)], first_self.at[t, h])

            wait(full.at[t, h, pl.ds(0, DEPTH // 2), :], twin_send.at[t, h])
            for d in range(2):
                wait(full.at[t, h, pl.ds(0, FEATS * 7 // 2), :], ring_send.at[t, h, d])
                three = full.at[t, h, pl.ds(0, 3 * HALF), pl.ds(0, PATCHES)]
                wait(three, rs_send.at[t, h, d])
                wait(three, ag_send.at[t, h, d])
        for stage in range(2):
            wait(heard.at[t, stage], norm_send.at[t, stage])
    combine_wait(1, sum_down, grad_down, 2)
    combine_wait(0, sum_up, grad_up, 4)


def on_device(inputs, cotangent, w_up, w_down, thresholds):
    x_t = jnp.swapaxes(inputs, 1, 2)
    dy_t = jnp.swapaxes(cotangent, 1, 2)
    vmem, hbm = pl.BlockSpec(memory_space=pltpu.VMEM), pl.BlockSpec(memory_space=pl.ANY)
    dma = pltpu.SemaphoreType.DMA
    return pl.pallas_call(
        kernel,
        out_shape=(
            jax.ShapeDtypeStruct((DEPTH, HIDDEN), F32),
            jax.ShapeDtypeStruct((HIDDEN, DEPTH), F32),
            jax.ShapeDtypeStruct((IMGS, 2), F32),
        ),
        in_specs=[vmem, vmem, hbm, hbm, pl.BlockSpec(memory_space=pltpu.SMEM)],
        out_specs=(hbm, hbm, vmem),
        scratch_shapes=[
            pltpu.VMEM((DEPTH, HIDDEN), BF16),
            pltpu.VMEM((2, HIDDEN, DEPTH), BF16),
            pltpu.VMEM((2, IMGS, DEPTH, WIDE), BF16),
            pltpu.VMEM((2, IMGS, NY, HIDDEN, PATCHES), BF16),
            pltpu.VMEM((2, IMGS, HIDDEN, PATCHES), F32),
            pltpu.VMEM((2, IMGS, 2, HALF, PATCHES), BF16),
            pltpu.VMEM((2, IMGS, 2, HIDDEN, PATCHES), BF16),
            pltpu.VMEM((IMGS, HIDDEN, PATCHES), F32),
            pltpu.VMEM((2, IMGS, NY, HIDDEN, PATCHES), BF16),
            pltpu.VMEM((COUNT, DEPTH, HIDDEN), BF16),
            pltpu.VMEM((COUNT, HIDDEN, DEPTH), BF16),
            pltpu.VMEM((DEPTH, HIDDEN), F32),
            pltpu.VMEM((HIDDEN, DEPTH), F32),
            pltpu.VMEM((2, COUNT, 128), F32),
            pltpu.VMEM((2, COUNT, 128), F32),
            pltpu.VMEM((2, 2, PEERS, COUNT, 128), F32),
            pltpu.VMEM((2, COUNT, 128), F32),
            pltpu.VMEM((2, COUNT, 128), F32),
            dma((2,)),
            dma((2, IMGS)),
            dma((2, IMGS)),
            dma((2, IMGS)),
            dma((2, IMGS, 2)),
            dma((2, IMGS, 2, NZ // 2)),
            dma((2, IMGS)),
            dma((2, IMGS)),
            dma((2, IMGS, 2)),
            dma((2, IMGS, 2, 3)),
            dma((2, IMGS, 2)),
            dma((2, IMGS, 2, 3)),
            dma((2, 2)),
            dma((2, 2)),
            dma((2, 4)),
        ],
        compiler_params=pltpu.CompilerParams(
            collective_id=0, has_side_effects=True, vmem_limit_bytes=66 * 2**20 - 2**21
        ),
        name="clipped_backward",
    )(x_t, dy_t, w_up, w_down, thresholds)


def solution(mesh):
    in_specs = (P("dp", None, "mp"), P("dp", None, "mp"), P("dp", "mp"), P("mp", "dp"), P())
    out_specs = (P("dp", "mp"), P("mp", "dp"), P("dp", None))
    return jax.shard_map(
        on_device, mesh=mesh, in_specs=in_specs, out_specs=out_specs, check_vma=False
    )
```
